32 devices in a mesh: ctx: 8 (over z, x), fsdp: 4 (over y, core).
Axes of the slice: x: 2, y: 2, z: 4, core: 2. Of those that a mesh axis runs over, the one named last changes fastest.
Arguments:
- inputs: bfloat16 [8, 512, 1024], P('fsdp', 'ctx'), may hold values from -6 to 6
- gain_one: bfloat16 [1024], P('fsdp'), may hold values from 0.25 to 1.75
- w_qkv: bfloat16 [1024, 3072], P('fsdp')
- w_attn: bfloat16 [1024, 1024], P('fsdp'), may hold values from -0.75 to 0.75
- gain_two: bfloat16 [1024], P('fsdp'), may hold values from 0.25 to 1.75
- w_in: bfloat16 [1024, 5248], P('fsdp'), may hold values from -0.1875 to 0.1875
- w_ffn: bfloat16 [2624, 1024], P('fsdp'), may hold values from -0.125 to 0.125
- cotangent: bfloat16 [8, 512, 1024], P('fsdp', 'ctx'), may hold values from -6 to 6
Outputs:
- output: bfloat16 [8, 512, 1024], P('fsdp', 'ctx')
- grad_input: float32 [8, 512, 1024], P('fsdp', 'ctx')
- grad_gain_one: float32 [1024], P('fsdp')
- grad_w_qkv: float32 [1024, 3072], P('fsdp')
- grad_w_attn: float32 [1024, 1024], P('fsdp')
- grad_gain_two: float32 [1024], P('fsdp')
- grad_w_in: float32 [1024, 5248], P('fsdp')
- grad_w_ffn: float32 [2624, 1024], P('fsdp')
The draws below stay inside these ranges and needn't reach their ends.
All inputs are finite; a program needn't handle non-finite values.
Results may differ from the reference program's by a relative error of at most 0.023.
Values may be sent and summed in bfloat16 or wider, within the bound.
A program may use at most 256 MiB of HBM per device.

```python
import math
import jax
import jax.numpy as jnp
from jax import lax

D = 1024
HEADS = 16
HEAD_DIM = 64
FF = 2624
LEN = 512
SEQS = 8


def draw_w_qkv(key, part):
    base_key = jax.random.fold_in(key, 11)
    keys_all = jax.random.split(base_key, 1)
    scale_in = D ** (-0.5)
    base_vals = jnp.clip(jax.random.normal(keys_all[0], (D, 3 * D), jnp.float32), -6.0, 6.0) * scale_in
    return base_vals.astype(jnp.bfloat16)


def steps_of(own_key, shape, cuts, smallest, high):
    level = 1.0
    for dim, parts in cuts:
        draws = jax.random.uniform(jax.random.fold_in(jax.random.fold_in(own_key, 6), dim), (parts,), jnp.float32, smallest / len(cuts), high / len(cuts))
        level = level * jnp.repeat(jnp.exp(draws), shape[dim] // parts).reshape((-1,) + (1,) * (len(shape) - 1 - dim))
    return level


def bell_draw(key, dims, scale, reach, pieces=(), held_as=jnp.bfloat16):
    values = scale * jax.random.normal(key, dims, jnp.float32)
    if pieces:
        values = values * steps_of(key, dims, pieces, -0.22, 0.18)
    return jnp.clip(values, -reach, reach).astype(held_as)


def setup_inputs(seed: int = 0) -> dict:
    key_of = jax.random.split(jax.random.key(seed), 9)
    return {
        "inputs": bell_draw(key_of[0], (SEQS, LEN, D), 1.0, 6.0, ((0, 4), (1, 8))),
        "gain_one": jnp.clip(1.0 + 0.15 * jax.random.normal(key_of[1], (D,), jnp.float32), 0.25, 1.75).astype(jnp.bfloat16),
        "w_qkv": draw_w_qkv(jax.random.fold_in(key_of[8], 71), 0),
        "w_attn": bell_draw(key_of[3], (D, D), (max(D * 32 // LEN, 1)) ** -0.5, 0.75, ((0, 4),)),
        "gain_two": jnp.clip(1.0 + 0.15 * jax.random.normal(key_of[4], (D,), jnp.float32), 0.25, 1.75).astype(jnp.bfloat16),
        "w_in": bell_draw(key_of[5], (D, 2 * FF), D ** -0.5, 0.1875, ((0, 4),)),
        "w_ffn": bell_draw(key_of[6], (FF, D), FF ** -0.5, 0.125, ((0, 4),)),
        "cotangent": bell_draw(key_of[7], (SEQS, LEN, D), 1.0, 6.0, ((0, 4), (1, 8))),
    }


EPSILON = 1e-05
ROPE_THETA = 160000.0

def to_half(values_in):
    return lax.optimization_barrier(values_in.astype(jnp.bfloat16))

def as_wide(values_in):
    return values_in.astype(jnp.float32)

def norm_parts(values_in):
    mean_val = lax.optimization_barrier(jnp.mean(values_in, axis=-1, keepdims=True))
    centred = values_in - mean_val
    variance = lax.optimization_barrier(jnp.mean(centred * centred, axis=-1, keepdims=True))
    inv_std = lax.rsqrt(variance + EPSILON)
    return (centred * inv_std, inv_std)

def norm_back(grad_normed, normed, inv_std):
    return inv_std * (grad_normed - lax.optimization_barrier(jnp.mean(grad_normed, axis=-1, keepdims=True)) - normed * lax.optimization_barrier(jnp.mean(grad_normed * normed, axis=-1, keepdims=True)))

def rotary_tables(positions):
    half_dim = HEAD_DIM // 2
    inv_freq = ROPE_THETA ** (-(jnp.arange(half_dim, dtype=jnp.float32) * 2.0) / HEAD_DIM)
    angles = positions.astype(jnp.float32)[:, None] * inv_freq[None, :]
    cosine = jnp.concatenate([jnp.cos(angles), jnp.cos(angles)], axis=-1)[:, None, :]
    sine_part = jnp.concatenate([jnp.sin(angles), jnp.sin(angles)], axis=-1)[:, None, :]
    return (cosine, sine_part)

def rotate(values_in, cosine, sine_part):
    half_dim = values_in.shape[-1] // 2
    turned = jnp.concatenate([-values_in[..., half_dim:], values_in[..., :half_dim]], axis=-1)
    return values_in * cosine + turned * sine_part

def rotate_back(grads, cosine, sine_part):
    half_dim = grads.shape[-1] // 2
    scaled = grads * sine_part
    turned = jnp.concatenate([scaled[..., half_dim:], -scaled[..., :half_dim]], axis=-1)
    return grads * cosine + turned

def gelu_slope(inner_part):
    cumulative = 0.5 * (1.0 + jax.scipy.special.erf(inner_part * 0.7071067811865476))
    density = jnp.exp(-0.5 * inner_part * inner_part) * 0.3989422804014327
    return cumulative + inner_part * density

def sequence_pass(tokens, grad_out, gain_one, w_qkv, w_attn, gain_two, w_in, w_ffn):
    length = tokens.shape[0]
    scale_factor = HEAD_DIM ** (-0.5)
    tokens_f = tokens.astype(jnp.float32)
    normed_one, inv_one = norm_parts(tokens_f)
    input_one = to_half(normed_one * gain_one.astype(jnp.float32))
    project = jnp.dot(input_one, w_qkv, preferred_element_type=jnp.float32)
    cosine, sine_part = rotary_tables(jnp.arange(length, dtype=jnp.int32))
    shaped = project.reshape(length, 3, HEADS, HEAD_DIM)
    queries = to_half(rotate(shaped[:, 0], cosine, sine_part))
    key_rows = to_half(rotate(shaped[:, 1], cosine, sine_part))
    value_rows = to_half(shaped[:, 2])
    keys_wide = as_wide(key_rows)
    values_wide = as_wide(value_rows)
    block_len = math.gcd(length, 512)
    blocks_num = length // block_len
    query_blocks = queries.reshape(blocks_num, block_len, HEADS, HEAD_DIM)

    def attend(query_block):
        scores = jnp.einsum('thd,shd->ths', as_wide(query_block), keys_wide) * scale_factor
        row_max = lax.optimization_barrier(jnp.max(scores, axis=-1))
        exp_vals = jnp.exp(scores - row_max[..., None])
        row_sum = lax.optimization_barrier(jnp.sum(exp_vals, axis=-1))
        weighted = jnp.einsum('ths,shd->thd', as_wide(to_half(exp_vals)), values_wide)
        return (weighted / row_sum[..., None], row_max + jnp.log(row_sum))
    attn_f, log_sum = lax.map(attend, query_blocks)
    attn_f = attn_f.reshape(length, HEADS, HEAD_DIM)
    log_sum = log_sum.reshape(length, HEADS)
    attn_b = to_half(attn_f.reshape(length, D))
    resid = tokens_f + jnp.dot(attn_b, w_attn, preferred_element_type=jnp.float32)
    normed_two, inv_two = norm_parts(resid)
    input_two = to_half(normed_two * gain_two.astype(jnp.float32))
    widened = jnp.dot(input_two, w_in, preferred_element_type=jnp.float32)
    inner_part = widened[:, :FF]
    gating = widened[:, FF:]
    activated = jax.nn.gelu(inner_part, approximate=False)
    hidden = to_half(activated * gating)
    output = (resid + jnp.dot(hidden, w_ffn, preferred_element_type=jnp.float32)).astype(jnp.bfloat16)
    grad_ffn = jnp.dot(hidden.T, grad_out, preferred_element_type=jnp.float32)
    grad_hidden = jnp.dot(grad_out, w_ffn.T, preferred_element_type=jnp.float32)
    grad_inner = grad_hidden * gating * gelu_slope(inner_part)
    grad_gating = grad_hidden * activated
    grad_wide = to_half(jnp.concatenate([grad_inner, grad_gating], axis=-1))
    grad_in = jnp.dot(input_two.T, grad_wide, preferred_element_type=jnp.float32)
    grad_normed_two = jnp.dot(grad_wide, w_in.T, preferred_element_type=jnp.float32)
    grad_g2 = lax.optimization_barrier(jnp.sum(grad_normed_two * normed_two, axis=0))
    grad_resid = grad_out.astype(jnp.float32) + norm_back(grad_normed_two * gain_two.astype(jnp.float32), normed_two, inv_two)
    resid_b = to_half(grad_resid)
    grad_attn_w = jnp.dot(attn_b.T, resid_b, preferred_element_type=jnp.float32)
    grad_mixed = to_half(jnp.dot(resid_b, w_attn.T, preferred_element_type=jnp.float32)).reshape(length, HEADS, HEAD_DIM)
    row_delta = lax.optimization_barrier(jnp.sum(as_wide(grad_mixed) * attn_f, axis=-1))

    def back(state_in, block_items):
        grad_key_all, grad_value_all = state_in
        query_block, grad_block, lse_block, delta_block = block_items
        scores = jnp.einsum('thd,shd->ths', as_wide(query_block), keys_wide) * scale_factor
        probs = jnp.exp(scores - lse_block[..., None])
        grad_value_all = grad_value_all + jnp.einsum('ths,thd->shd', as_wide(to_half(probs)), as_wide(grad_block))
        grad_probs = jnp.einsum('thd,shd->ths', as_wide(grad_block), values_wide)
        grad_scores = as_wide(to_half(probs * (grad_probs - delta_block[..., None])))
        grad_query = jnp.einsum('ths,shd->thd', grad_scores, keys_wide) * scale_factor
        grad_key_all = grad_key_all + jnp.einsum('ths,thd->shd', grad_scores, as_wide(query_block)) * scale_factor
        return ((grad_key_all, grad_value_all), grad_query)
    zero_kv = jnp.zeros((length, HEADS, HEAD_DIM), jnp.float32)
    block_items = (query_blocks, grad_mixed.reshape(blocks_num, block_len, HEADS, HEAD_DIM), log_sum.reshape(blocks_num, block_len, HEADS), row_delta.reshape(blocks_num, block_len, HEADS))
    (grad_key_all, grad_value_all), grad_query = lax.scan(back, (zero_kv, zero_kv), block_items)
    grad_query = grad_query.reshape(length, HEADS, HEAD_DIM)
    grad_q_rot = rotate_back(grad_query, cosine, sine_part).reshape(length, D)
    grad_k_rot = rotate_back(grad_key_all, cosine, sine_part).reshape(length, D)
    grad_joint = to_half(jnp.concatenate([grad_q_rot, grad_k_rot, grad_value_all.reshape(length, D)], axis=-1))
    grad_qkv = jnp.dot(input_one.T, grad_joint, preferred_element_type=jnp.float32)
    grad_normed_one = jnp.dot(grad_joint, w_qkv.T, preferred_element_type=jnp.float32)
    grad_g1 = lax.optimization_barrier(jnp.sum(grad_normed_one * normed_one, axis=0))
    grad_input = grad_resid + norm_back(grad_normed_one * gain_one.astype(jnp.float32), normed_one, inv_one)
    return (output, grad_input, (grad_g1, grad_qkv, grad_attn_w, grad_g2, grad_in, grad_ffn))

def reference(inputs, gain_one, w_qkv, w_attn, gain_two, w_in, w_ffn, cotangent):

    def step(state_in, pair):
        output, grad_input, grads = sequence_pass(pair[0], pair[1], gain_one, w_qkv, w_attn, gain_two, w_in, w_ffn)
        return (tuple((before + added for before, added in zip(state_in, grads))), (output, grad_input))
    zeros_all = (jnp.zeros((D,), jnp.float32), jnp.zeros((D, 3 * D), jnp.float32), jnp.zeros((D, D), jnp.float32), jnp.zeros((D,), jnp.float32), jnp.zeros((D, 2 * FF), jnp.float32), jnp.zeros((FF, D), jnp.float32))
    grads, (outputs, grad_inputs) = lax.scan(step, zeros_all, (inputs, cotangent))
    return (outputs, grad_inputs, grads[0], grads[1], grads[2], grads[3], grads[4], grads[5])
```

```python
import math

import jax
import jax.numpy as jnp
from jax import lax
from jax.sharding import PartitionSpec as P

D = 1024
HEADS = 16
HEAD_DIM = 64
FF = 2624


EPSILON = 1e-05
ROPE_THETA = 160000.0


def norm_parts(values_in):
    mean_val = jnp.mean(values_in, axis=-1, keepdims=True)
    centred = values_in - mean_val
    variance = jnp.mean(centred * centred, axis=-1, keepdims=True)
    inv_std = lax.rsqrt(variance + EPSILON)
    return (centred * inv_std, inv_std)


def norm_back(grad_normed, normed, inv_std):
    return inv_std * (
        grad_normed
        - jnp.mean(grad_normed, axis=-1, keepdims=True)
        - normed * jnp.mean(grad_normed * normed, axis=-1, keepdims=True)
    )


def rotary_tables(positions):
    half_dim = HEAD_DIM // 2
    inv_freq = ROPE_THETA ** (-(jnp.arange(half_dim, dtype=jnp.float32) * 2.0) / HEAD_DIM)
    angles = positions.astype(jnp.float32)[:, None] * inv_freq[None, :]
    cosine = jnp.concatenate([jnp.cos(angles), jnp.cos(angles)], axis=-1)[:, None, :]
    sine_part = jnp.concatenate([jnp.sin(angles), jnp.sin(angles)], axis=-1)[:, None, :]
    return (cosine, sine_part)


def rotate(values_in, cosine, sine_part):
    half_dim = values_in.shape[-1] // 2
    turned = jnp.concatenate([-values_in[..., half_dim:], values_in[..., :half_dim]], axis=-1)
    return values_in * cosine + turned * sine_part


def rotate_back(grads, cosine, sine_part):
    half_dim = grads.shape[-1] // 2
    scaled = grads * sine_part
    turned = jnp.concatenate([scaled[..., half_dim:], -scaled[..., :half_dim]], axis=-1)
    return grads * cosine + turned


def gelu_slope(inner_part):
    cumulative = 0.5 * (1.0 + jax.scipy.special.erf(inner_part * 0.7071067811865476))
    density = jnp.exp(-0.5 * inner_part * inner_part) * 0.3989422804014327
    return cumulative + inner_part * density


def attend_piece(state_in, queries, key_piece, value_piece, scale_factor):
    row_max, row_sum, weighted = state_in
    scores = (
        jnp.einsum("bthd,bshd->bths", queries, key_piece, preferred_element_type=jnp.float32)
        * scale_factor
    )
    new_max = jnp.maximum(row_max, jnp.max(scores, axis=-1))
    rescale = jnp.exp(row_max - new_max)
    exp_vals = jnp.exp(scores - new_max[..., None])
    row_sum = row_sum * rescale + jnp.sum(exp_vals, axis=-1)
    weighted = weighted * rescale[..., None] + jnp.einsum(
        "bths,bshd->bthd",
        exp_vals.astype(jnp.bfloat16),
        value_piece,
        preferred_element_type=jnp.float32,
    )
    return (new_max, row_sum, weighted)


def back_piece(queries, grad_mixed, log_sum, row_delta, key_piece, value_piece, scale_factor):
    scores = (
        jnp.einsum("bthd,bshd->bths", queries, key_piece, preferred_element_type=jnp.float32)
        * scale_factor
    )
    probs = jnp.exp(scores - log_sum[..., None])
    grad_values = jnp.einsum(
        "bths,bthd->bshd",
        probs.astype(jnp.bfloat16),
        grad_mixed,
        preferred_element_type=jnp.float32,
    )
    grad_probs = jnp.einsum(
        "bthd,bshd->bths", grad_mixed, value_piece, preferred_element_type=jnp.float32
    )
    grad_scores = (probs * (grad_probs - row_delta[..., None])).astype(jnp.bfloat16)
    grad_query = (
        jnp.einsum("bths,bshd->bthd", grad_scores, key_piece, preferred_element_type=jnp.float32)
        * scale_factor
    )
    grad_keys = (
        jnp.einsum("bths,bthd->bshd", grad_scores, queries, preferred_element_type=jnp.float32)
        * scale_factor
    )
    return (grad_query, grad_keys, grad_values)


def add_at(whole_grads, piece_grads, offset):
    old_part = lax.dynamic_slice_in_dim(whole_grads, offset, piece_grads.shape[1], 1)
    return lax.dynamic_update_slice_in_dim(whole_grads, old_part + piece_grads, offset, 1)


def on_device(inputs, gain_one, w_qkv, w_attn, gain_two, w_in, w_ffn, cotangent):
    seq_dev = inputs.shape[0]
    tok_seq = inputs.shape[1]
    row_count = seq_dev * tok_seq
    seq_len = tok_seq * lax.axis_size("ctx")
    tokens_f = inputs.reshape(row_count, D).astype(jnp.float32)
    grad_out = cotangent.reshape(row_count, D)
    scale_factor = HEAD_DIM ** (-0.5)
    block_len = math.gcd(seq_len, 512)
    blocks_num = seq_len // block_len
    gathered = (
        lax.all_gather(gain_one, "fsdp", axis=0, tiled=True),
        lax.all_gather(w_qkv, "fsdp", axis=0, tiled=True),
        lax.all_gather(w_attn, "fsdp", axis=0, tiled=True),
        lax.all_gather(gain_two, "fsdp", axis=0, tiled=True),
        lax.all_gather(w_in, "fsdp", axis=0, tiled=True),
        lax.all_gather(w_ffn, "fsdp", axis=0, tiled=True),
    )
    full_g1, full_qkv, full_attn, full_g2, full_in, full_ffn = gathered
    normed_one, inv_one = norm_parts(tokens_f)
    input_one = (normed_one * full_g1.astype(jnp.float32)).astype(jnp.bfloat16)
    project = jnp.dot(input_one, full_qkv, preferred_element_type=jnp.float32)
    positions = lax.axis_index("ctx") * tok_seq + jnp.arange(tok_seq, dtype=jnp.int32)
    cosine, sine_part = rotary_tables(positions)
    shaped = project.reshape(seq_dev, tok_seq, 3, HEADS, HEAD_DIM)
    queries = rotate(shaped[:, :, 0], cosine, sine_part).astype(jnp.bfloat16)
    key_rows = rotate(shaped[:, :, 1], cosine, sine_part).astype(jnp.bfloat16)
    value_rows = shaped[:, :, 2].astype(jnp.bfloat16)
    start_state = (
        jnp.full((seq_dev, tok_seq, HEADS), -jnp.inf, jnp.float32),
        jnp.zeros((seq_dev, tok_seq, HEADS), jnp.float32),
        jnp.zeros((seq_dev, tok_seq, HEADS, HEAD_DIM), jnp.float32),
    )
    whole_keys, whole_values = (
        lax.all_gather(key_rows, "ctx", axis=1, tiled=True),
        lax.all_gather(value_rows, "ctx", axis=1, tiled=True),
    )

    def forward_step(state_in, block_index):
        begin = block_index * block_len
        key_piece = lax.dynamic_slice_in_dim(whole_keys, begin, block_len, 1)
        value_piece = lax.dynamic_slice_in_dim(whole_values, begin, block_len, 1)
        return (attend_piece(state_in, queries, key_piece, value_piece, scale_factor), None)

    state_out, unused = lax.scan(forward_step, start_state, jnp.arange(blocks_num, dtype=jnp.int32))
    row_max, row_sum, weighted = state_out
    attn_f = weighted / row_sum[..., None]
    log_sum = row_max + jnp.log(row_sum)
    attn_b = attn_f.reshape(row_count, D).astype(jnp.bfloat16)
    resid = tokens_f + jnp.dot(attn_b, full_attn, preferred_element_type=jnp.float32)
    normed_two, inv_two = norm_parts(resid)
    input_two = (normed_two * full_g2.astype(jnp.float32)).astype(jnp.bfloat16)
    widened = jnp.dot(input_two, full_in, preferred_element_type=jnp.float32)
    inner_part = widened[:, :FF]
    gating = widened[:, FF:]
    activated = jax.nn.gelu(inner_part, approximate=False)
    hidden = (activated * gating).astype(jnp.bfloat16)
    output = (resid + jnp.dot(hidden, full_ffn, preferred_element_type=jnp.float32)).astype(
        jnp.bfloat16
    )
    back_g1, back_qkv, back_attn, back_g2, back_in, back_ffn = gathered
    grad_ffn = jnp.dot(hidden.T, grad_out, preferred_element_type=jnp.float32)
    grad_hidden = jnp.dot(grad_out, back_ffn.T, preferred_element_type=jnp.float32)
    grad_inner = grad_hidden * gating * gelu_slope(inner_part)
    grad_gating = grad_hidden * activated
    grad_wide = jnp.concatenate([grad_inner, grad_gating], axis=-1).astype(jnp.bfloat16)
    grad_in = jnp.dot(input_two.T, grad_wide, preferred_element_type=jnp.float32)
    grad_normed_two = jnp.dot(grad_wide, back_in.T, preferred_element_type=jnp.float32)
    grad_g2 = jnp.sum(grad_normed_two * normed_two, axis=0)
    grad_resid = grad_out.astype(jnp.float32) + norm_back(
        grad_normed_two * back_g2.astype(jnp.float32), normed_two, inv_two
    )
    part_g2, part_in, part_ffn = (
        lax.psum_scatter(
            grad_g2.astype(jnp.bfloat16), "fsdp", scatter_dimension=0, tiled=True
        ).astype(jnp.float32),
        lax.psum_scatter(
            grad_in.astype(jnp.bfloat16), "fsdp", scatter_dimension=0, tiled=True
        ).astype(jnp.float32),
        lax.psum_scatter(
            grad_ffn.astype(jnp.bfloat16), "fsdp", scatter_dimension=0, tiled=True
        ).astype(jnp.float32),
    )
    resid_b = grad_resid.astype(jnp.bfloat16)
    grad_attn_w = jnp.dot(attn_b.T, resid_b, preferred_element_type=jnp.float32)
    grad_mixed = (
        jnp.dot(resid_b, back_attn.T, preferred_element_type=jnp.float32)
        .astype(jnp.bfloat16)
        .reshape(seq_dev, tok_seq, HEADS, HEAD_DIM)
    )
    row_delta = jnp.sum(grad_mixed.astype(jnp.float32) * attn_f, axis=-1)
    zero_q = jnp.zeros((seq_dev, tok_seq, HEADS, HEAD_DIM), jnp.float32)
    zero_kv = jnp.zeros((seq_dev, seq_len, HEADS, HEAD_DIM), jnp.float32)

    def backward_step(state_in, block_index):
        grad_q_sum, grad_key_all, grad_value_all = state_in
        begin = block_index * block_len
        key_piece = lax.dynamic_slice_in_dim(whole_keys, begin, block_len, 1)
        value_piece = lax.dynamic_slice_in_dim(whole_values, begin, block_len, 1)
        grad_query, grad_keys, grad_values = back_piece(
            queries, grad_mixed, log_sum, row_delta, key_piece, value_piece, scale_factor
        )
        return (
            (
                grad_q_sum + grad_query,
                add_at(grad_key_all, grad_keys, begin),
                add_at(grad_value_all, grad_values, begin),
            ),
            None,
        )

    back_state, unused_back = lax.scan(
        backward_step, (zero_q, zero_kv, zero_kv), jnp.arange(blocks_num, dtype=jnp.int32)
    )
    grad_q_sum, grad_key_all, grad_value_all = back_state
    own_keys, own_values = (
        lax.psum_scatter(
            grad_key_all.astype(jnp.bfloat16), "ctx", scatter_dimension=1, tiled=True
        ).astype(jnp.float32),
        lax.psum_scatter(
            grad_value_all.astype(jnp.bfloat16), "ctx", scatter_dimension=1, tiled=True
        ).astype(jnp.float32),
    )
    grad_q_rot = rotate_back(grad_q_sum, cosine, sine_part).reshape(row_count, D)
    grad_k_rot = rotate_back(own_keys, cosine, sine_part).reshape(row_count, D)
    grad_joint = jnp.concatenate(
        [grad_q_rot, grad_k_rot, own_values.reshape(row_count, D)], axis=-1
    ).astype(jnp.bfloat16)
    grad_qkv = jnp.dot(input_one.T, grad_joint, preferred_element_type=jnp.float32)
    grad_normed_one = jnp.dot(grad_joint, back_qkv.T, preferred_element_type=jnp.float32)
    grad_g1 = jnp.sum(grad_normed_one * normed_one, axis=0)
    grad_input = grad_resid + norm_back(
        grad_normed_one * back_g1.astype(jnp.float32), normed_one, inv_one
    )
    part_g1, part_qkv, part_attn = (
        lax.psum_scatter(
            grad_g1.astype(jnp.bfloat16), "fsdp", scatter_dimension=0, tiled=True
        ).astype(jnp.float32),
        lax.psum_scatter(
            grad_qkv.astype(jnp.bfloat16), "fsdp", scatter_dimension=0, tiled=True
        ).astype(jnp.float32),
        lax.psum_scatter(
            grad_attn_w.astype(jnp.bfloat16), "fsdp", scatter_dimension=0, tiled=True
        ).astype(jnp.float32),
    )
    totals = (
        lax.psum(part_g1.astype(jnp.bfloat16), "ctx").astype(jnp.float32),
        lax.psum(part_qkv.astype(jnp.bfloat16), "ctx").astype(jnp.float32),
        lax.psum(part_attn.astype(jnp.bfloat16), "ctx").astype(jnp.float32),
        lax.psum(part_g2.astype(jnp.bfloat16), "ctx").astype(jnp.float32),
        lax.psum(part_in.astype(jnp.bfloat16), "ctx").astype(jnp.float32),
        lax.psum(part_ffn.astype(jnp.bfloat16), "ctx").astype(jnp.float32),
    )
    return (
        output.reshape(seq_dev, tok_seq, D),
        grad_input.reshape(seq_dev, tok_seq, D),
        totals[0],
        totals[1],
        totals[2],
        totals[3],
        totals[4],
        totals[5],
    )


def gather_tokens(rows):
    return lax.all_gather(rows, "ctx", axis=0, tiled=True)


def scatter_tokens(partial_rows):
    return lax.psum_scatter(
        partial_rows.astype(jnp.bfloat16), "ctx", scatter_dimension=0, tiled=True
    ).astype(jnp.float32)


def by_heads(inputs, gain_one, w_qkv, w_attn, gain_two, w_in, w_ffn, cotangent):
    blocks = lax.axis_size("ctx")
    owners = lax.axis_size("fsdp")
    block = lax.axis_index("ctx")
    seq_dev, tok_seq, _ = inputs.shape
    own_rows = seq_dev * tok_seq
    all_rows = own_rows * blocks
    seq_len = tok_seq * blocks
    row_part = w_qkv.shape[0]
    head_cols = D // blocks
    heads_dev = HEADS // blocks
    unit_dev = FF // blocks
    scale_factor = HEAD_DIM ** (-0.5)
    f32, bf16 = jnp.float32, jnp.bfloat16

    own_x = inputs.reshape(own_rows, D)
    own_cot = cotangent.reshape(own_rows, D)

    qkv_part = lax.dynamic_slice_in_dim(
        w_qkv.reshape(row_part, 3, D), block * head_cols, head_cols, 2
    ).reshape(row_part, 3 * head_cols)
    in_part = jnp.concatenate(
        [
            lax.dynamic_slice_in_dim(w_in, block * unit_dev, unit_dev, 1),
            lax.dynamic_slice_in_dim(w_in, FF + block * unit_dev, unit_dev, 1),
        ],
        axis=1,
    )
    packed = jnp.concatenate([qkv_part, gain_one[:, None], gain_two[:, None]], axis=1)
    packed = lax.all_gather(packed, "fsdp", axis=0, tiled=True)
    qkv_c = packed[:, : 3 * head_cols]
    full_g1 = packed[:, 3 * head_cols].astype(f32)
    full_g2 = packed[:, 3 * head_cols + 1].astype(f32)
    all_x = gather_tokens(own_x)
    full_attn = lax.all_gather(w_attn, "fsdp", axis=0, tiled=True)
    in_c = lax.all_gather(in_part, "fsdp", axis=0, tiled=True)
    ffn_cols = lax.all_to_all(w_ffn, "fsdp", split_axis=1, concat_axis=0, tiled=True)
    ffn_c = lax.all_gather(
        lax.dynamic_slice_in_dim(ffn_cols, block * unit_dev, unit_dev, 0),
        "fsdp",
        axis=1,
        tiled=True,
    )
    all_cot = gather_tokens(own_cot)

    normed_all, _ = norm_parts(all_x.astype(f32))
    input_one = (normed_all * full_g1).astype(bf16)
    project = jnp.dot(input_one, qkv_c, preferred_element_type=f32)
    cosine, sine_part = rotary_tables(jnp.arange(seq_len, dtype=jnp.int32))
    shaped = project.reshape(blocks, seq_dev, tok_seq, 3, heads_dev, HEAD_DIM)
    shaped = shaped.transpose(3, 1, 0, 2, 4, 5).reshape(3, seq_dev, seq_len, heads_dev, HEAD_DIM)
    queries = rotate(shaped[0], cosine, sine_part).astype(bf16)
    key_rows = rotate(shaped[1], cosine, sine_part).astype(bf16)
    value_rows = shaped[2].astype(bf16)
    scores = (
        jnp.einsum("bthd,bshd->bhts", queries, key_rows, preferred_element_type=f32) * scale_factor
    )
    row_max = jnp.max(scores, axis=-1, keepdims=True)
    exp_vals = jnp.exp(scores - row_max)
    row_sum = jnp.sum(exp_vals, axis=-1, keepdims=True)
    weighted = jnp.einsum(
        "bhts,bshd->bhtd", exp_vals.astype(bf16), value_rows, preferred_element_type=f32
    )
    attn_f = weighted / row_sum
    log_sum = row_max + jnp.log(row_sum)
    attn_b = attn_f.astype(bf16).reshape(seq_dev, heads_dev, blocks, tok_seq, HEAD_DIM)
    attn_b = attn_b.transpose(2, 0, 3, 1, 4).reshape(blocks, own_rows, head_cols)
    own_attn = lax.all_to_all(attn_b, "ctx", split_axis=0, concat_axis=0, tiled=True)
    own_attn = own_attn.transpose(1, 0, 2).reshape(own_rows, D)

    resid = own_x.astype(f32) + jnp.dot(own_attn, full_attn, preferred_element_type=f32)
    normed_two, inv_two = norm_parts(resid)
    input_two = gather_tokens((normed_two * full_g2).astype(bf16))

    widened = jnp.dot(input_two, in_c, preferred_element_type=f32)
    inner_part = widened[:, :unit_dev]
    gating = widened[:, unit_dev:]
    activated = jax.nn.gelu(inner_part, approximate=False)
    hidden = (activated * gating).astype(bf16)
    grad_hidden = lax.dot_general(
        all_cot, ffn_c, (((1,), (1,)), ((), ())), preferred_element_type=f32
    )
    grad_wide = jnp.concatenate(
        [grad_hidden * gating * gelu_slope(inner_part), grad_hidden * activated], axis=-1
    ).astype(bf16)
    own_grad_two = scatter_tokens(
        lax.dot_general(grad_wide, in_c, (((1,), (1,)), ((), ())), preferred_element_type=f32)
    )
    output = resid + scatter_tokens(jnp.dot(hidden, ffn_c, preferred_element_type=f32))

    grad_in = lax.dot_general(
        grad_wide, input_two, (((0,), (0,)), ((), ())), preferred_element_type=f32
    ).astype(bf16)
    grad_in = lax.psum_scatter(grad_in, "fsdp", scatter_dimension=1, tiled=True)
    grad_in = lax.all_gather(grad_in, "ctx", axis=0, tiled=False)
    grad_in = grad_in.reshape(blocks, 2, unit_dev, row_part).transpose(1, 0, 2, 3)
    grad_in = grad_in.reshape(2 * FF, row_part).T.astype(f32)
    grad_ffn = lax.dot_general(
        hidden, all_cot, (((0,), (0,)), ((), ())), preferred_element_type=f32
    ).astype(bf16)
    grad_ffn = lax.psum_scatter(grad_ffn, "fsdp", scatter_dimension=1, tiled=True)
    grad_ffn = lax.all_gather(grad_ffn, "ctx", axis=0, tiled=True)
    grad_ffn = lax.all_to_all(grad_ffn, "fsdp", split_axis=0, concat_axis=1, tiled=True)
    grad_ffn = grad_ffn.astype(f32)

    own_resid = own_cot.astype(f32) + norm_back(own_grad_two * full_g2, normed_two, inv_two)
    resid_b = own_resid.astype(bf16)
    own_mixed = lax.dot_general(
        resid_b, full_attn, (((1,), (1,)), ((), ())), preferred_element_type=f32
    ).astype(bf16)
    own_mixed = own_mixed.reshape(own_rows, blocks, head_cols).transpose(1, 0, 2)
    mixed = lax.all_to_all(own_mixed, "ctx", split_axis=0, concat_axis=0, tiled=True)
    mixed = mixed.reshape(blocks, seq_dev, tok_seq, heads_dev, HEAD_DIM).transpose(1, 3, 0, 2, 4)
    mixed = mixed.reshape(seq_dev, heads_dev, seq_len, HEAD_DIM)
    grad_attn = lax.dot_general(
        own_attn, resid_b, (((0,), (0,)), ((), ())), preferred_element_type=f32
    ).astype(bf16)
    grad_attn = lax.psum_scatter(grad_attn, "fsdp", scatter_dimension=0, tiled=True)
    grad_attn = lax.psum(grad_attn, "ctx").astype(f32)

    row_delta = jnp.sum(mixed.astype(f32) * attn_f, axis=-1, keepdims=True)
    probs = jnp.exp(scores - log_sum)
    grad_values = jnp.einsum(
        "bhts,bhtd->bshd", probs.astype(bf16), mixed, preferred_element_type=f32
    )
    grad_probs = jnp.einsum("bhtd,bshd->bhts", mixed, value_rows, preferred_element_type=f32)
    grad_scores = (probs * (grad_probs - row_delta)).astype(bf16)
    grad_query = (
        jnp.einsum("bhts,bshd->bthd", grad_scores, key_rows, preferred_element_type=f32)
        * scale_factor
    )
    grad_keys = (
        jnp.einsum("bhts,bthd->bshd", grad_scores, queries, preferred_element_type=f32)
        * scale_factor
    )
    joint = jnp.stack(
        [
            rotate_back(grad_query, cosine, sine_part),
            rotate_back(grad_keys, cosine, sine_part),
            grad_values,
        ]
    ).astype(bf16)
    joint = joint.reshape(3, seq_dev, blocks, tok_seq, head_cols).transpose(2, 1, 3, 0, 4)
    joint = joint.reshape(all_rows, 3 * head_cols)
    own_grad_one = scatter_tokens(
        lax.dot_general(joint, qkv_c, (((1,), (1,)), ((), ())), preferred_element_type=f32)
    )
    grad_qkv = lax.dot_general(
        input_one, joint, (((0,), (0,)), ((), ())), preferred_element_type=f32
    ).astype(bf16)
    grad_qkv = lax.psum_scatter(grad_qkv, "fsdp", scatter_dimension=0, tiled=True)
    grad_qkv = lax.all_gather(grad_qkv, "ctx", axis=0, tiled=False)
    grad_qkv = grad_qkv.reshape(blocks, row_part, 3, head_cols).transpose(1, 2, 0, 3)
    grad_qkv = grad_qkv.reshape(row_part, 3 * D).astype(f32)
    normed_one, inv_one = norm_parts(own_x.astype(f32))
    grad_input = own_resid + norm_back(own_grad_one * full_g1, normed_one, inv_one)

    grad_g1 = jnp.sum(w_qkv.astype(f32) * grad_qkv, axis=1) / gain_one.astype(f32)
    grad_g2 = jnp.sum(w_in.astype(f32) * grad_in, axis=1) / gain_two.astype(f32)
    return (
        output.astype(bf16).reshape(seq_dev, tok_seq, D),
        grad_input.reshape(seq_dev, tok_seq, D),
        grad_g1,
        grad_qkv,
        grad_attn,
        grad_g2,
        grad_in,
        grad_ffn,
    )


def solution(mesh):
    blocks = mesh.shape["ctx"]
    split_ok = HEADS % blocks == 0 and FF % blocks == 0 and (D // blocks) % 128 == 0

    return jax.shard_map(
        by_heads if split_ok else on_device,
        mesh=mesh,
        in_specs=(
            P("fsdp", "ctx", None),
            P("fsdp"),
            P("fsdp", None),
            P("fsdp", None),
            P("fsdp"),
            P("fsdp", None),
            P("fsdp", None),
            P("fsdp", "ctx", None),
        ),
        out_specs=(
            P("fsdp", "ctx", None),
            P("fsdp", "ctx", None),
            P("fsdp"),
            P("fsdp", None),
            P("fsdp", None),
            P("fsdp"),
            P("fsdp", None),
            P("fsdp", None),
        ),
        check_vma=False,
    )
```

```python
import math

import jax
import jax.numpy as jnp
from jax import lax
from jax.sharding import PartitionSpec as P

D = 1024
HEADS = 16
HEAD_DIM = 64
FF = 2624


EPSILON = 1e-05
ROPE_THETA = 160000.0


def norm_parts(values_in):
    mean_val = jnp.mean(values_in, axis=-1, keepdims=True)
    centred = values_in - mean_val
    variance = jnp.mean(centred * centred, axis=-1, keepdims=True)
    inv_std = lax.rsqrt(variance + EPSILON)
    return (centred * inv_std, inv_std)


def norm_back(grad_normed, normed, inv_std):
    return inv_std * (
        grad_normed
        - jnp.mean(grad_normed, axis=-1, keepdims=True)
        - normed * jnp.mean(grad_normed * normed, axis=-1, keepdims=True)
    )


def rotary_tables(positions):
    half_dim = HEAD_DIM // 2
    inv_freq = ROPE_THETA ** (-(jnp.arange(half_dim, dtype=jnp.float32) * 2.0) / HEAD_DIM)
    angles = positions.astype(jnp.float32)[:, None] * inv_freq[None, :]
    cosine = jnp.concatenate([jnp.cos(angles), jnp.cos(angles)], axis=-1)[:, None, :]
    sine_part = jnp.concatenate([jnp.sin(angles), jnp.sin(angles)], axis=-1)[:, None, :]
    return (cosine, sine_part)


def rotate(values_in, cosine, sine_part):
    half_dim = values_in.shape[-1] // 2
    turned = jnp.concatenate([-values_in[..., half_dim:], values_in[..., :half_dim]], axis=-1)
    return values_in * cosine + turned * sine_part


def rotate_back(grads, cosine, sine_part):
    half_dim = grads.shape[-1] // 2
    scaled = grads * sine_part
    turned = jnp.concatenate([scaled[..., half_dim:], -scaled[..., :half_dim]], axis=-1)
    return grads * cosine + turned


def gelu_slope(inner_part):
    cumulative = 0.5 * (1.0 + jax.scipy.special.erf(inner_part * 0.7071067811865476))
    density = jnp.exp(-0.5 * inner_part * inner_part) * 0.3989422804014327
    return cumulative + inner_part * density


def attend_piece(state_in, queries, key_piece, value_piece, scale_factor):
    row_max, row_sum, weighted = state_in
    scores = (
        jnp.einsum("bthd,bshd->bths", queries, key_piece, preferred_element_type=jnp.float32)
        * scale_factor
    )
    new_max = jnp.maximum(row_max, jnp.max(scores, axis=-1))
    rescale = jnp.exp(row_max - new_max)
    exp_vals = jnp.exp(scores - new_max[..., None])
    row_sum = row_sum * rescale + jnp.sum(exp_vals, axis=-1)
    weighted = weighted * rescale[..., None] + jnp.einsum(
        "bths,bshd->bthd",
        exp_vals.astype(jnp.bfloat16),
        value_piece,
        preferred_element_type=jnp.float32,
    )
    return (new_max, row_sum, weighted)


def back_piece(queries, grad_mixed, log_sum, row_delta, key_piece, value_piece, scale_factor):
    scores = (
        jnp.einsum("bthd,bshd->bths", queries, key_piece, preferred_element_type=jnp.float32)
        * scale_factor
    )
    probs = jnp.exp(scores - log_sum[..., None])
    grad_values = jnp.einsum(
        "bths,bthd->bshd",
        probs.astype(jnp.bfloat16),
        grad_mixed,
        preferred_element_type=jnp.float32,
    )
    grad_probs = jnp.einsum(
        "bthd,bshd->bths", grad_mixed, value_piece, preferred_element_type=jnp.float32
    )
    grad_scores = (probs * (grad_probs - row_delta[..., None])).astype(jnp.bfloat16)
    grad_query = (
        jnp.einsum("bths,bshd->bthd", grad_scores, key_piece, preferred_element_type=jnp.float32)
        * scale_factor
    )
    grad_keys = (
        jnp.einsum("bths,bthd->bshd", grad_scores, queries, preferred_element_type=jnp.float32)
        * scale_factor
    )
    return (grad_query, grad_keys, grad_values)


def add_at(whole_grads, piece_grads, offset):
    old_part = lax.dynamic_slice_in_dim(whole_grads, offset, piece_grads.shape[1], 1)
    return lax.dynamic_update_slice_in_dim(whole_grads, old_part + piece_grads, offset, 1)


def on_device(inputs, gain_one, w_qkv, w_attn, gain_two, w_in, w_ffn, cotangent):
    seq_dev = inputs.shape[0]
    tok_seq = inputs.shape[1]
    row_count = seq_dev * tok_seq
    seq_len = tok_seq * lax.axis_size("ctx")
    tokens_f = inputs.reshape(row_count, D).astype(jnp.float32)
    grad_out = cotangent.reshape(row_count, D)
    scale_factor = HEAD_DIM ** (-0.5)
    block_len = math.gcd(seq_len, 512)
    blocks_num = seq_len // block_len
    gathered = (
        lax.all_gather(gain_one, "fsdp", axis=0, tiled=True),
        lax.all_gather(w_qkv, "fsdp", axis=0, tiled=True),
        lax.all_gather(w_attn, "fsdp", axis=0, tiled=True),
        lax.all_gather(gain_two, "fsdp", axis=0, tiled=True),
        lax.all_gather(w_in, "fsdp", axis=0, tiled=True),
        lax.all_gather(w_ffn, "fsdp", axis=0, tiled=True),
    )
    full_g1, full_qkv, full_attn, full_g2, full_in, full_ffn = gathered
    normed_one, inv_one = norm_parts(tokens_f)
    input_one = (normed_one * full_g1.astype(jnp.float32)).astype(jnp.bfloat16)
    project = jnp.dot(input_one, full_qkv, preferred_element_type=jnp.float32)
    positions = lax.axis_index("ctx") * tok_seq + jnp.arange(tok_seq, dtype=jnp.int32)
    cosine, sine_part = rotary_tables(positions)
    shaped = project.reshape(seq_dev, tok_seq, 3, HEADS, HEAD_DIM)
    queries = rotate(shaped[:, :, 0], cosine, sine_part).astype(jnp.bfloat16)
    key_rows = rotate(shaped[:, :, 1], cosine, sine_part).astype(jnp.bfloat16)
    value_rows = shaped[:, :, 2].astype(jnp.bfloat16)
    start_state = (
        jnp.full((seq_dev, tok_seq, HEADS), -jnp.inf, jnp.float32),
        jnp.zeros((seq_dev, tok_seq, HEADS), jnp.float32),
        jnp.zeros((seq_dev, tok_seq, HEADS, HEAD_DIM), jnp.float32),
    )
    whole_keys, whole_values = (
        lax.all_gather(key_rows, "ctx", axis=1, tiled=True),
        lax.all_gather(value_rows, "ctx", axis=1, tiled=True),
    )

    def forward_step(state_in, block_index):
        begin = block_index * block_len
        key_piece = lax.dynamic_slice_in_dim(whole_keys, begin, block_len, 1)
        value_piece = lax.dynamic_slice_in_dim(whole_values, begin, block_len, 1)
        return (attend_piece(state_in, queries, key_piece, value_piece, scale_factor), None)

    state_out, unused = lax.scan(forward_step, start_state, jnp.arange(blocks_num, dtype=jnp.int32))
    row_max, row_sum, weighted = state_out
    attn_f = weighted / row_sum[..., None]
    log_sum = row_max + jnp.log(row_sum)
    attn_b = attn_f.reshape(row_count, D).astype(jnp.bfloat16)
    resid = tokens_f + jnp.dot(attn_b, full_attn, preferred_element_type=jnp.float32)
    normed_two, inv_two = norm_parts(resid)
    input_two = (normed_two * full_g2.astype(jnp.float32)).astype(jnp.bfloat16)
    widened = jnp.dot(input_two, full_in, preferred_element_type=jnp.float32)
    inner_part = widened[:, :FF]
    gating = widened[:, FF:]
    activated = jax.nn.gelu(inner_part, approximate=False)
    hidden = (activated * gating).astype(jnp.bfloat16)
    output = (resid + jnp.dot(hidden, full_ffn, preferred_element_type=jnp.float32)).astype(
        jnp.bfloat16
    )
    back_g1, back_qkv, back_attn, back_g2, back_in, back_ffn = gathered
    grad_ffn = jnp.dot(hidden.T, grad_out, preferred_element_type=jnp.float32)
    grad_hidden = jnp.dot(grad_out, back_ffn.T, preferred_element_type=jnp.float32)
    grad_inner = grad_hidden * gating * gelu_slope(inner_part)
    grad_gating = grad_hidden * activated
    grad_wide = jnp.concatenate([grad_inner, grad_gating], axis=-1).astype(jnp.bfloat16)
    grad_in = jnp.dot(input_two.T, grad_wide, preferred_element_type=jnp.float32)
    grad_normed_two = jnp.dot(grad_wide, back_in.T, preferred_element_type=jnp.float32)
    grad_g2 = jnp.sum(grad_normed_two * normed_two, axis=0)
    grad_resid = grad_out.astype(jnp.float32) + norm_back(
        grad_normed_two * back_g2.astype(jnp.float32), normed_two, inv_two
    )
    part_g2, part_in, part_ffn = (
        lax.psum_scatter(
            grad_g2.astype(jnp.bfloat16), "fsdp", scatter_dimension=0, tiled=True
        ).astype(jnp.float32),
        lax.psum_scatter(
            grad_in.astype(jnp.bfloat16), "fsdp", scatter_dimension=0, tiled=True
        ).astype(jnp.float32),
        lax.psum_scatter(
            grad_ffn.astype(jnp.bfloat16), "fsdp", scatter_dimension=0, tiled=True
        ).astype(jnp.float32),
    )
    resid_b = grad_resid.astype(jnp.bfloat16)
    grad_attn_w = jnp.dot(attn_b.T, resid_b, preferred_element_type=jnp.float32)
    grad_mixed = (
        jnp.dot(resid_b, back_attn.T, preferred_element_type=jnp.float32)
        .astype(jnp.bfloat16)
        .reshape(seq_dev, tok_seq, HEADS, HEAD_DIM)
    )
    row_delta = jnp.sum(grad_mixed.astype(jnp.float32) * attn_f, axis=-1)
    zero_q = jnp.zeros((seq_dev, tok_seq, HEADS, HEAD_DIM), jnp.float32)
    zero_kv = jnp.zeros((seq_dev, seq_len, HEADS, HEAD_DIM), jnp.float32)

    def backward_step(state_in, block_index):
        grad_q_sum, grad_key_all, grad_value_all = state_in
        begin = block_index * block_len
        key_piece = lax.dynamic_slice_in_dim(whole_keys, begin, block_len, 1)
        value_piece = lax.dynamic_slice_in_dim(whole_values, begin, block_len, 1)
        grad_query, grad_keys, grad_values = back_piece(
            queries, grad_mixed, log_sum, row_delta, key_piece, value_piece, scale_factor
        )
        return (
            (
                grad_q_sum + grad_query,
                add_at(grad_key_all, grad_keys, begin),
                add_at(grad_value_all, grad_values, begin),
            ),
            None,
        )

    back_state, unused_back = lax.scan(
        backward_step, (zero_q, zero_kv, zero_kv), jnp.arange(blocks_num, dtype=jnp.int32)
    )
    grad_q_sum, grad_key_all, grad_value_all = back_state
    own_keys, own_values = (
        lax.psum_scatter(
            grad_key_all.astype(jnp.bfloat16), "ctx", scatter_dimension=1, tiled=True
        ).astype(jnp.float32),
        lax.psum_scatter(
            grad_value_all.astype(jnp.bfloat16), "ctx", scatter_dimension=1, tiled=True
        ).astype(jnp.float32),
    )
    grad_q_rot = rotate_back(grad_q_sum, cosine, sine_part).reshape(row_count, D)
    grad_k_rot = rotate_back(own_keys, cosine, sine_part).reshape(row_count, D)
    grad_joint = jnp.concatenate(
        [grad_q_rot, grad_k_rot, own_values.reshape(row_count, D)], axis=-1
    ).astype(jnp.bfloat16)
    grad_qkv = jnp.dot(input_one.T, grad_joint, preferred_element_type=jnp.float32)
    grad_normed_one = jnp.dot(grad_joint, back_qkv.T, preferred_element_type=jnp.float32)
    grad_g1 = jnp.sum(grad_normed_one * normed_one, axis=0)
    grad_input = grad_resid + norm_back(
        grad_normed_one * back_g1.astype(jnp.float32), normed_one, inv_one
    )
    part_g1, part_qkv, part_attn = (
        lax.psum_scatter(
            grad_g1.astype(jnp.bfloat16), "fsdp", scatter_dimension=0, tiled=True
        ).astype(jnp.float32),
        lax.psum_scatter(
            grad_qkv.astype(jnp.bfloat16), "fsdp", scatter_dimension=0, tiled=True
        ).astype(jnp.float32),
        lax.psum_scatter(
            grad_attn_w.astype(jnp.bfloat16), "fsdp", scatter_dimension=0, tiled=True
        ).astype(jnp.float32),
    )
    totals = (
        lax.psum(part_g1.astype(jnp.bfloat16), "ctx").astype(jnp.float32),
        lax.psum(part_qkv.astype(jnp.bfloat16), "ctx").astype(jnp.float32),
        lax.psum(part_attn.astype(jnp.bfloat16), "ctx").astype(jnp.float32),
        lax.psum(part_g2.astype(jnp.bfloat16), "ctx").astype(jnp.float32),
        lax.psum(part_in.astype(jnp.bfloat16), "ctx").astype(jnp.float32),
        lax.psum(part_ffn.astype(jnp.bfloat16), "ctx").astype(jnp.float32),
    )
    return (
        output.reshape(seq_dev, tok_seq, D),
        grad_input.reshape(seq_dev, tok_seq, D),
        totals[0],
        totals[1],
        totals[2],
        totals[3],
        totals[4],
        totals[5],
    )


def ring_order(blocks):
    return list(range(0, blocks, 2)) + list(range(blocks - 1, 0, -2))


def ring_moves(blocks):
    order = ring_order(blocks)
    ahead = [(order[i], order[(i + 1) % blocks]) for i in range(blocks)]
    return ahead, [(after, before) for before, after in ahead]


def gather_tokens(rows):
    blocks = lax.axis_size("ctx")
    half, cut = blocks // 2, rows.shape[0] // 2
    ahead, behind = ring_moves(blocks)
    found = [rows] + [None] * (blocks - 1)
    from_before = from_after = rows
    for step in range(1, half):
        from_before = lax.ppermute(from_before, "ctx", ahead)
        from_after = lax.ppermute(from_after, "ctx", behind)
        found[blocks - step] = from_before
        found[step] = from_after
    found[half] = jnp.concatenate(
        [
            lax.ppermute(from_before[:cut], "ctx", ahead),
            lax.ppermute(from_after[cut:], "ctx", behind),
        ]
    )
    return jnp.concatenate(found)


def scatter_tokens(partial_rows):
    blocks = lax.axis_size("ctx")
    half = blocks // 2
    rows = partial_rows.shape[0] // blocks
    cut = rows // 2
    ahead, behind = ring_moves(blocks)
    terms = [partial_rows[i * rows : (i + 1) * rows] for i in range(blocks)]
    to_ahead = lax.ppermute(terms[half][:cut].astype(jnp.bfloat16), "ctx", ahead)
    to_behind = lax.ppermute(terms[half][cut:].astype(jnp.bfloat16), "ctx", behind)
    for step in range(half - 1, 0, -1):
        to_ahead, to_behind = to_ahead.astype(jnp.float32), to_behind.astype(jnp.float32)
        if step == half - 1:
            to_ahead = jnp.concatenate([to_ahead, jnp.zeros_like(to_ahead)])
            to_behind = jnp.concatenate([jnp.zeros_like(to_behind), to_behind])
        to_ahead = (terms[step] + to_ahead).astype(jnp.bfloat16)
        to_behind = (terms[blocks - step] + to_behind).astype(jnp.bfloat16)
        to_ahead = lax.ppermute(to_ahead, "ctx", ahead)
        to_behind = lax.ppermute(to_behind, "ctx", behind)
    return terms[0] + to_ahead.astype(jnp.float32) + to_behind.astype(jnp.float32)


def by_heads(inputs, gain_one, w_qkv, w_attn, gain_two, w_in, w_ffn, cotangent):
    blocks = lax.axis_size("ctx")
    owners = lax.axis_size("fsdp")
    block = lax.axis_index("ctx")
    seq_dev, tok_seq, _ = inputs.shape
    own_rows = seq_dev * tok_seq
    all_rows = own_rows * blocks
    seq_len = tok_seq * blocks
    row_part = w_qkv.shape[0]
    head_cols = D // blocks
    heads_dev = HEADS // blocks
    unit_dev = FF // blocks
    scale_factor = HEAD_DIM ** (-0.5)
    f32, bf16 = jnp.float32, jnp.bfloat16

    order = ring_order(blocks)
    places = jnp.array([order.index(i) for i in range(blocks)], jnp.int32)
    place = places[block]
    ring_block = jnp.array(order, jnp.int32)[(place + jnp.arange(blocks)) % blocks]
    positions = ring_block[:, None] * tok_seq + jnp.arange(tok_seq, dtype=jnp.int32)[None, :]

    own_x = inputs.reshape(own_rows, D)
    own_cot = cotangent.reshape(own_rows, D)

    qkv_part = lax.dynamic_slice_in_dim(
        w_qkv.reshape(row_part, 3, D), block * head_cols, head_cols, 2
    ).reshape(row_part, 3 * head_cols)
    in_part = jnp.concatenate(
        [
            lax.dynamic_slice_in_dim(w_in, block * unit_dev, unit_dev, 1),
            lax.dynamic_slice_in_dim(w_in, FF + block * unit_dev, unit_dev, 1),
        ],
        axis=1,
    )
    packed = jnp.concatenate([qkv_part, gain_one[:, None], gain_two[:, None]], axis=1)
    packed = lax.all_gather(packed, "fsdp", axis=0, tiled=True)
    qkv_c = packed[:, : 3 * head_cols]
    full_g1 = packed[:, 3 * head_cols].astype(f32)
    full_g2 = packed[:, 3 * head_cols + 1].astype(f32)
    all_x = gather_tokens(own_x)
    full_attn = lax.all_gather(w_attn, "fsdp", axis=0, tiled=True)
    in_c = lax.all_gather(in_part, "fsdp", axis=0, tiled=True)
    ffn_cols = lax.all_to_all(w_ffn, "fsdp", split_axis=1, concat_axis=0, tiled=True)
    ffn_c = lax.all_gather(
        lax.dynamic_slice_in_dim(ffn_cols, block * unit_dev, unit_dev, 0),
        "fsdp",
        axis=1,
        tiled=True,
    )
    all_cot = gather_tokens(own_cot)

    normed_all, _ = norm_parts(all_x.astype(f32))
    input_one = (normed_all * full_g1).astype(bf16)
    project = jnp.dot(input_one, qkv_c, preferred_element_type=f32)
    cosine, sine_part = rotary_tables(positions.reshape(seq_len))
    shaped = project.reshape(blocks, seq_dev, tok_seq, 3, heads_dev, HEAD_DIM)
    shaped = shaped.transpose(3, 1, 0, 2, 4, 5).reshape(3, seq_dev, seq_len, heads_dev, HEAD_DIM)
    queries = rotate(shaped[0], cosine, sine_part).astype(bf16)
    key_rows = rotate(shaped[1], cosine, sine_part).astype(bf16)
    value_rows = shaped[2].astype(bf16)
    scores = (
        jnp.einsum("bthd,bshd->bhts", queries, key_rows, preferred_element_type=f32) * scale_factor
    )
    row_max = jnp.max(scores, axis=-1, keepdims=True)
    exp_vals = jnp.exp(scores - row_max)
    row_sum = jnp.sum(exp_vals, axis=-1, keepdims=True)
    weighted = jnp.einsum(
        "bhts,bshd->bhtd", exp_vals.astype(bf16), value_rows, preferred_element_type=f32
    )
    attn_f = weighted / row_sum
    log_sum = row_max + jnp.log(row_sum)
    attn_b = attn_f.astype(bf16).reshape(seq_dev, heads_dev, blocks, tok_seq, HEAD_DIM)
    attn_b = attn_b.transpose(2, 0, 3, 1, 4).reshape(blocks, own_rows, head_cols)
    by_block = jnp.take(attn_b, (places - place) % blocks, axis=0)
    own_attn = lax.all_to_all(by_block, "ctx", split_axis=0, concat_axis=0, tiled=True)
    own_attn = own_attn.transpose(1, 0, 2).reshape(own_rows, D)

    resid = own_x.astype(f32) + jnp.dot(own_attn, full_attn, preferred_element_type=f32)
    normed_two, inv_two = norm_parts(resid)
    input_two = gather_tokens((normed_two * full_g2).astype(bf16))

    widened = jnp.dot(input_two, in_c, preferred_element_type=f32)
    inner_part = widened[:, :unit_dev]
    gating = widened[:, unit_dev:]
    activated = jax.nn.gelu(inner_part, approximate=False)
    hidden = (activated * gating).astype(bf16)
    grad_hidden = lax.dot_general(
        all_cot, ffn_c, (((1,), (1,)), ((), ())), preferred_element_type=f32
    )
    grad_wide = jnp.concatenate(
        [grad_hidden * gating * gelu_slope(inner_part), grad_hidden * activated], axis=-1
    ).astype(bf16)
    own_grad_two = scatter_tokens(
        lax.dot_general(grad_wide, in_c, (((1,), (1,)), ((), ())), preferred_element_type=f32)
    )
    output = resid + scatter_tokens(jnp.dot(hidden, ffn_c, preferred_element_type=f32))

    grad_in = lax.dot_general(
        grad_wide, input_two, (((0,), (0,)), ((), ())), preferred_element_type=f32
    ).astype(bf16)
    grad_in = lax.psum_scatter(grad_in, "fsdp", scatter_dimension=1, tiled=True)
    grad_in = lax.all_gather(grad_in, "ctx", axis=0, tiled=False)
    grad_in = grad_in.reshape(blocks, 2, unit_dev, row_part).transpose(1, 0, 2, 3)
    grad_in = grad_in.reshape(2 * FF, row_part).T.astype(f32)
    grad_ffn = lax.dot_general(
        hidden, all_cot, (((0,), (0,)), ((), ())), preferred_element_type=f32
    ).astype(bf16)
    grad_ffn = lax.psum_scatter(grad_ffn, "fsdp", scatter_dimension=1, tiled=True)
    grad_ffn = lax.all_gather(grad_ffn, "ctx", axis=0, tiled=True)
    grad_ffn = lax.all_to_all(grad_ffn, "fsdp", split_axis=0, concat_axis=1, tiled=True)
    grad_ffn = grad_ffn.astype(f32)

    own_resid = own_cot.astype(f32) + norm_back(own_grad_two * full_g2, normed_two, inv_two)
    resid_b = own_resid.astype(bf16)
    all_resid = gather_tokens(resid_b)
    attn_c = lax.dynamic_slice_in_dim(full_attn, block * head_cols, head_cols, 0)
    mixed = lax.dot_general(
        all_resid, attn_c, (((1,), (1,)), ((), ())), preferred_element_type=f32
    ).astype(bf16)
    mixed = mixed.reshape(blocks, seq_dev, tok_seq, heads_dev, HEAD_DIM).transpose(1, 3, 0, 2, 4)
    mixed = mixed.reshape(seq_dev, heads_dev, seq_len, HEAD_DIM)
    grad_attn = lax.dot_general(
        attn_b.reshape(all_rows, head_cols),
        all_resid,
        (((0,), (0,)), ((), ())),
        preferred_element_type=f32,
    ).astype(bf16)

    row_delta = jnp.sum(mixed.astype(f32) * attn_f, axis=-1, keepdims=True)
    probs = jnp.exp(scores - log_sum)
    grad_values = jnp.einsum(
        "bhts,bhtd->bshd", probs.astype(bf16), mixed, preferred_element_type=f32
    )
    grad_probs = jnp.einsum("bhtd,bshd->bhts", mixed, value_rows, preferred_element_type=f32)
    grad_scores = (probs * (grad_probs - row_delta)).astype(bf16)
    grad_query = (
        jnp.einsum("bhts,bshd->bthd", grad_scores, key_rows, preferred_element_type=f32)
        * scale_factor
    )
    grad_keys = (
        jnp.einsum("bhts,bthd->bshd", grad_scores, queries, preferred_element_type=f32)
        * scale_factor
    )
    joint = jnp.stack(
        [
            rotate_back(grad_query, cosine, sine_part),
            rotate_back(grad_keys, cosine, sine_part),
            grad_values,
        ]
    ).astype(bf16)
    joint = joint.reshape(3, seq_dev, blocks, tok_seq, head_cols).transpose(2, 1, 3, 0, 4)
    joint = joint.reshape(all_rows, 3 * head_cols)
    own_grad_one = scatter_tokens(
        lax.dot_general(joint, qkv_c, (((1,), (1,)), ((), ())), preferred_element_type=f32)
    )
    grad_qkv = lax.dot_general(
        joint, input_one, (((0,), (0,)), ((), ())), preferred_element_type=f32
    ).astype(bf16)
    grads = jnp.concatenate([grad_qkv, grad_attn])
    grads = lax.psum_scatter(grads, "fsdp", scatter_dimension=1, tiled=True)
    grads = lax.all_gather(grads, "ctx", axis=0, tiled=False)
    grad_qkv = grads[:, : 3 * head_cols].reshape(blocks, 3, head_cols, row_part)
    grad_qkv = grad_qkv.transpose(1, 0, 2, 3).reshape(3 * D, row_part).T.astype(f32)
    grad_attn = grads[:, 3 * head_cols :].reshape(D, row_part)
    grad_attn = lax.all_to_all(grad_attn, "fsdp", split_axis=0, concat_axis=1, tiled=True)
    grad_attn = grad_attn.astype(f32)
    normed_one, inv_one = norm_parts(own_x.astype(f32))
    grad_input = own_resid + norm_back(own_grad_one * full_g1, normed_one, inv_one)

    grad_g1 = jnp.sum(w_qkv.astype(f32) * grad_qkv, axis=1) / gain_one.astype(f32)
    grad_g2 = jnp.sum(w_in.astype(f32) * grad_in, axis=1) / gain_two.astype(f32)
    return (
        output.astype(bf16).reshape(seq_dev, tok_seq, D),
        grad_input.reshape(seq_dev, tok_seq, D),
        grad_g1,
        grad_qkv,
        grad_attn,
        grad_g2,
        grad_in,
        grad_ffn,
    )


def solution(mesh):
    blocks = mesh.shape["ctx"]
    split_ok = blocks % 4 == 0 and HEADS % blocks == 0 and FF % blocks == 0 and (D // blocks) % 128 == 0

    return jax.shard_map(
        by_heads if split_ok else on_device,
        mesh=mesh,
        in_specs=(
            P("fsdp", "ctx", None),
            P("fsdp"),
            P("fsdp", None),
            P("fsdp", None),
            P("fsdp"),
            P("fsdp", None),
            P("fsdp", None),
            P("fsdp", "ctx", None),
        ),
        out_specs=(
            P("fsdp", "ctx", None),
            P("fsdp", "ctx", None),
            P("fsdp"),
            P("fsdp", None),
            P("fsdp", None),
            P("fsdp"),
            P("fsdp", None),
            P("fsdp", None),
        ),
        check_vma=False,
    )
```

```python
import math

import jax
import jax.numpy as jnp
from jax import lax
from jax.sharding import PartitionSpec as P

D = 1024
HEADS = 16
HEAD_DIM = 64
FF = 2624


EPSILON = 1e-05
ROPE_THETA = 160000.0


def norm_parts(values_in):
    mean_val = jnp.mean(values_in, axis=-1, keepdims=True)
    centred = values_in - mean_val
    variance = jnp.mean(centred * centred, axis=-1, keepdims=True)
    inv_std = lax.rsqrt(variance + EPSILON)
    return (centred * inv_std, inv_std)


def norm_back(grad_normed, normed, inv_std):
    return inv_std * (
        grad_normed
        - jnp.mean(grad_normed, axis=-1, keepdims=True)
        - normed * jnp.mean(grad_normed * normed, axis=-1, keepdims=True)
    )


def rotary_tables(positions):
    half_dim = HEAD_DIM // 2
    inv_freq = ROPE_THETA ** (-(jnp.arange(half_dim, dtype=jnp.float32) * 2.0) / HEAD_DIM)
    angles = positions.astype(jnp.float32)[:, None] * inv_freq[None, :]
    cosine = jnp.concatenate([jnp.cos(angles), jnp.cos(angles)], axis=-1)[:, None, :]
    sine_part = jnp.concatenate([jnp.sin(angles), jnp.sin(angles)], axis=-1)[:, None, :]
    return (cosine, sine_part)


def rotate(values_in, cosine, sine_part):
    half_dim = values_in.shape[-1] // 2
    turned = jnp.concatenate([-values_in[..., half_dim:], values_in[..., :half_dim]], axis=-1)
    return values_in * cosine + turned * sine_part


def rotate_back(grads, cosine, sine_part):
    half_dim = grads.shape[-1] // 2
    scaled = grads * sine_part
    turned = jnp.concatenate([scaled[..., half_dim:], -scaled[..., :half_dim]], axis=-1)
    return grads * cosine + turned


def gelu_slope(inner_part):
    cumulative = 0.5 * (1.0 + jax.scipy.special.erf(inner_part * 0.7071067811865476))
    density = jnp.exp(-0.5 * inner_part * inner_part) * 0.3989422804014327
    return cumulative + inner_part * density


def attend_piece(state_in, queries, key_piece, value_piece, scale_factor):
    row_max, row_sum, weighted = state_in
    scores = (
        jnp.einsum("bthd,bshd->bths", queries, key_piece, preferred_element_type=jnp.float32)
        * scale_factor
    )
    new_max = jnp.maximum(row_max, jnp.max(scores, axis=-1))
    rescale = jnp.exp(row_max - new_max)
    exp_vals = jnp.exp(scores - new_max[..., None])
    row_sum = row_sum * rescale + jnp.sum(exp_vals, axis=-1)
    weighted = weighted * rescale[..., None] + jnp.einsum(
        "bths,bshd->bthd",
        exp_vals.astype(jnp.bfloat16),
        value_piece,
        preferred_element_type=jnp.float32,
    )
    return (new_max, row_sum, weighted)


def back_piece(queries, grad_mixed, log_sum, row_delta, key_piece, value_piece, scale_factor):
    scores = (
        jnp.einsum("bthd,bshd->bths", queries, key_piece, preferred_element_type=jnp.float32)
        * scale_factor
    )
    probs = jnp.exp(scores - log_sum[..., None])
    grad_values = jnp.einsum(
        "bths,bthd->bshd",
        probs.astype(jnp.bfloat16),
        grad_mixed,
        preferred_element_type=jnp.float32,
    )
    grad_probs = jnp.einsum(
        "bthd,bshd->bths", grad_mixed, value_piece, preferred_element_type=jnp.float32
    )
    grad_scores = (probs * (grad_probs - row_delta[..., None])).astype(jnp.bfloat16)
    grad_query = (
        jnp.einsum("bths,bshd->bthd", grad_scores, key_piece, preferred_element_type=jnp.float32)
        * scale_factor
    )
    grad_keys = (
        jnp.einsum("bths,bthd->bshd", grad_scores, queries, preferred_element_type=jnp.float32)
        * scale_factor
    )
    return (grad_query, grad_keys, grad_values)


def add_at(whole_grads, piece_grads, offset):
    old_part = lax.dynamic_slice_in_dim(whole_grads, offset, piece_grads.shape[1], 1)
    return lax.dynamic_update_slice_in_dim(whole_grads, old_part + piece_grads, offset, 1)


def on_device(inputs, gain_one, w_qkv, w_attn, gain_two, w_in, w_ffn, cotangent):
    seq_dev = inputs.shape[0]
    tok_seq = inputs.shape[1]
    row_count = seq_dev * tok_seq
    seq_len = tok_seq * lax.axis_size("ctx")
    tokens_f = inputs.reshape(row_count, D).astype(jnp.float32)
    grad_out = cotangent.reshape(row_count, D)
    scale_factor = HEAD_DIM ** (-0.5)
    block_len = math.gcd(seq_len, 512)
    blocks_num = seq_len // block_len
    gathered = (
        lax.all_gather(gain_one, "fsdp", axis=0, tiled=True),
        lax.all_gather(w_qkv, "fsdp", axis=0, tiled=True),
        lax.all_gather(w_attn, "fsdp", axis=0, tiled=True),
        lax.all_gather(gain_two, "fsdp", axis=0, tiled=True),
        lax.all_gather(w_in, "fsdp", axis=0, tiled=True),
        lax.all_gather(w_ffn, "fsdp", axis=0, tiled=True),
    )
    full_g1, full_qkv, full_attn, full_g2, full_in, full_ffn = gathered
    normed_one, inv_one = norm_parts(tokens_f)
    input_one = (normed_one * full_g1.astype(jnp.float32)).astype(jnp.bfloat16)
    project = jnp.dot(input_one, full_qkv, preferred_element_type=jnp.float32)
    positions = lax.axis_index("ctx") * tok_seq + jnp.arange(tok_seq, dtype=jnp.int32)
    cosine, sine_part = rotary_tables(positions)
    shaped = project.reshape(seq_dev, tok_seq, 3, HEADS, HEAD_DIM)
    queries = rotate(shaped[:, :, 0], cosine, sine_part).astype(jnp.bfloat16)
    key_rows = rotate(shaped[:, :, 1], cosine, sine_part).astype(jnp.bfloat16)
    value_rows = shaped[:, :, 2].astype(jnp.bfloat16)
    start_state = (
        jnp.full((seq_dev, tok_seq, HEADS), -jnp.inf, jnp.float32),
        jnp.zeros((seq_dev, tok_seq, HEADS), jnp.float32),
        jnp.zeros((seq_dev, tok_seq, HEADS, HEAD_DIM), jnp.float32),
    )
    whole_keys, whole_values = (
        lax.all_gather(key_rows, "ctx", axis=1, tiled=True),
        lax.all_gather(value_rows, "ctx", axis=1, tiled=True),
    )

    def forward_step(state_in, block_index):
        begin = block_index * block_len
        key_piece = lax.dynamic_slice_in_dim(whole_keys, begin, block_len, 1)
        value_piece = lax.dynamic_slice_in_dim(whole_values, begin, block_len, 1)
        return (attend_piece(state_in, queries, key_piece, value_piece, scale_factor), None)

    state_out, unused = lax.scan(forward_step, start_state, jnp.arange(blocks_num, dtype=jnp.int32))
    row_max, row_sum, weighted = state_out
    attn_f = weighted / row_sum[..., None]
    log_sum = row_max + jnp.log(row_sum)
    attn_b = attn_f.reshape(row_count, D).astype(jnp.bfloat16)
    resid = tokens_f + jnp.dot(attn_b, full_attn, preferred_element_type=jnp.float32)
    normed_two, inv_two = norm_parts(resid)
    input_two = (normed_two * full_g2.astype(jnp.float32)).astype(jnp.bfloat16)
    widened = jnp.dot(input_two, full_in, preferred_element_type=jnp.float32)
    inner_part = widened[:, :FF]
    gating = widened[:, FF:]
    activated = jax.nn.gelu(inner_part, approximate=False)
    hidden = (activated * gating).astype(jnp.bfloat16)
    output = (resid + jnp.dot(hidden, full_ffn, preferred_element_type=jnp.float32)).astype(
        jnp.bfloat16
    )
    back_g1, back_qkv, back_attn, back_g2, back_in, back_ffn = gathered
    grad_ffn = jnp.dot(hidden.T, grad_out, preferred_element_type=jnp.float32)
    grad_hidden = jnp.dot(grad_out, back_ffn.T, preferred_element_type=jnp.float32)
    grad_inner = grad_hidden * gating * gelu_slope(inner_part)
    grad_gating = grad_hidden * activated
    grad_wide = jnp.concatenate([grad_inner, grad_gating], axis=-1).astype(jnp.bfloat16)
    grad_in = jnp.dot(input_two.T, grad_wide, preferred_element_type=jnp.float32)
    grad_normed_two = jnp.dot(grad_wide, back_in.T, preferred_element_type=jnp.float32)
    grad_g2 = jnp.sum(grad_normed_two * normed_two, axis=0)
    grad_resid = grad_out.astype(jnp.float32) + norm_back(
        grad_normed_two * back_g2.astype(jnp.float32), normed_two, inv_two
    )
    part_g2, part_in, part_ffn = (
        lax.psum_scatter(
            grad_g2.astype(jnp.bfloat16), "fsdp", scatter_dimension=0, tiled=True
        ).astype(jnp.float32),
        lax.psum_scatter(
            grad_in.astype(jnp.bfloat16), "fsdp", scatter_dimension=0, tiled=True
        ).astype(jnp.float32),
        lax.psum_scatter(
            grad_ffn.astype(jnp.bfloat16), "fsdp", scatter_dimension=0, tiled=True
        ).astype(jnp.float32),
    )
    resid_b = grad_resid.astype(jnp.bfloat16)
    grad_attn_w = jnp.dot(attn_b.T, resid_b, preferred_element_type=jnp.float32)
    grad_mixed = (
        jnp.dot(resid_b, back_attn.T, preferred_element_type=jnp.float32)
        .astype(jnp.bfloat16)
        .reshape(seq_dev, tok_seq, HEADS, HEAD_DIM)
    )
    row_delta = jnp.sum(grad_mixed.astype(jnp.float32) * attn_f, axis=-1)
    zero_q = jnp.zeros((seq_dev, tok_seq, HEADS, HEAD_DIM), jnp.float32)
    zero_kv = jnp.zeros((seq_dev, seq_len, HEADS, HEAD_DIM), jnp.float32)

    def backward_step(state_in, block_index):
        grad_q_sum, grad_key_all, grad_value_all = state_in
        begin = block_index * block_len
        key_piece = lax.dynamic_slice_in_dim(whole_keys, begin, block_len, 1)
        value_piece = lax.dynamic_slice_in_dim(whole_values, begin, block_len, 1)
        grad_query, grad_keys, grad_values = back_piece(
            queries, grad_mixed, log_sum, row_delta, key_piece, value_piece, scale_factor
        )
        return (
            (
                grad_q_sum + grad_query,
                add_at(grad_key_all, grad_keys, begin),
                add_at(grad_value_all, grad_values, begin),
            ),
            None,
        )

    back_state, unused_back = lax.scan(
        backward_step, (zero_q, zero_kv, zero_kv), jnp.arange(blocks_num, dtype=jnp.int32)
    )
    grad_q_sum, grad_key_all, grad_value_all = back_state
    own_keys, own_values = (
        lax.psum_scatter(
            grad_key_all.astype(jnp.bfloat16), "ctx", scatter_dimension=1, tiled=True
        ).astype(jnp.float32),
        lax.psum_scatter(
            grad_value_all.astype(jnp.bfloat16), "ctx", scatter_dimension=1, tiled=True
        ).astype(jnp.float32),
    )
    grad_q_rot = rotate_back(grad_q_sum, cosine, sine_part).reshape(row_count, D)
    grad_k_rot = rotate_back(own_keys, cosine, sine_part).reshape(row_count, D)
    grad_joint = jnp.concatenate(
        [grad_q_rot, grad_k_rot, own_values.reshape(row_count, D)], axis=-1
    ).astype(jnp.bfloat16)
    grad_qkv = jnp.dot(input_one.T, grad_joint, preferred_element_type=jnp.float32)
    grad_normed_one = jnp.dot(grad_joint, back_qkv.T, preferred_element_type=jnp.float32)
    grad_g1 = jnp.sum(grad_normed_one * normed_one, axis=0)
    grad_input = grad_resid + norm_back(
        grad_normed_one * back_g1.astype(jnp.float32), normed_one, inv_one
    )
    part_g1, part_qkv, part_attn = (
        lax.psum_scatter(
            grad_g1.astype(jnp.bfloat16), "fsdp", scatter_dimension=0, tiled=True
        ).astype(jnp.float32),
        lax.psum_scatter(
            grad_qkv.astype(jnp.bfloat16), "fsdp", scatter_dimension=0, tiled=True
        ).astype(jnp.float32),
        lax.psum_scatter(
            grad_attn_w.astype(jnp.bfloat16), "fsdp", scatter_dimension=0, tiled=True
        ).astype(jnp.float32),
    )
    totals = (
        lax.psum(part_g1.astype(jnp.bfloat16), "ctx").astype(jnp.float32),
        lax.psum(part_qkv.astype(jnp.bfloat16), "ctx").astype(jnp.float32),
        lax.psum(part_attn.astype(jnp.bfloat16), "ctx").astype(jnp.float32),
        lax.psum(part_g2.astype(jnp.bfloat16), "ctx").astype(jnp.float32),
        lax.psum(part_in.astype(jnp.bfloat16), "ctx").astype(jnp.float32),
        lax.psum(part_ffn.astype(jnp.bfloat16), "ctx").astype(jnp.float32),
    )
    return (
        output.reshape(seq_dev, tok_seq, D),
        grad_input.reshape(seq_dev, tok_seq, D),
        totals[0],
        totals[1],
        totals[2],
        totals[3],
        totals[4],
        totals[5],
    )


def ring_order(blocks):
    return list(range(0, blocks, 2)) + list(range(blocks - 1, 0, -2))


def ring_moves(blocks):
    order = ring_order(blocks)
    ahead = [(order[i], order[(i + 1) % blocks]) for i in range(blocks)]
    return ahead, [(after, before) for before, after in ahead]


def gather_tokens(rows):
    blocks = lax.axis_size("ctx")
    half, cut = blocks // 2, rows.shape[0] // 32 * 16
    ahead, behind = ring_moves(blocks)
    found = [rows] + [None] * (blocks - 1)
    from_before = from_after = rows
    for step in range(1, half):
        from_before = lax.ppermute(from_before, "ctx", ahead)
        from_after = lax.ppermute(from_after, "ctx", behind)
        found[blocks - step] = from_before
        found[step] = from_after
    found[half] = jnp.concatenate(
        [
            lax.ppermute(from_before[:cut], "ctx", ahead),
            lax.ppermute(from_after[cut:], "ctx", behind),
        ]
    )
    return jnp.concatenate(found)


def scatter_tokens(partial_rows):
    blocks = lax.axis_size("ctx")
    half = blocks // 2
    rows = partial_rows.shape[0] // blocks
    cut = rows // 2
    ahead, behind = ring_moves(blocks)
    terms = [partial_rows[i * rows : (i + 1) * rows] for i in range(blocks)]
    to_ahead = lax.ppermute(terms[half][:cut].astype(jnp.bfloat16), "ctx", ahead)
    to_behind = lax.ppermute(terms[half][cut:].astype(jnp.bfloat16), "ctx", behind)
    for step in range(half - 1, 0, -1):
        to_ahead, to_behind = to_ahead.astype(jnp.float32), to_behind.astype(jnp.float32)
        if step == half - 1:
            to_ahead = jnp.concatenate([to_ahead, jnp.zeros_like(to_ahead)])
            to_behind = jnp.concatenate([jnp.zeros_like(to_behind), to_behind])
        to_ahead = (terms[step] + to_ahead).astype(jnp.bfloat16)
        to_behind = (terms[blocks - step] + to_behind).astype(jnp.bfloat16)
        to_ahead = lax.ppermute(to_ahead, "ctx", ahead)
        to_behind = lax.ppermute(to_behind, "ctx", behind)
    return terms[0] + to_ahead.astype(jnp.float32) + to_behind.astype(jnp.float32)


def by_heads(inputs, gain_one, w_qkv, w_attn, gain_two, w_in, w_ffn, cotangent):
    blocks = lax.axis_size("ctx")
    owners = lax.axis_size("fsdp")
    block = lax.axis_index("ctx")
    seq_dev, tok_seq, _ = inputs.shape
    own_rows = seq_dev * tok_seq
    all_rows = own_rows * blocks
    seq_len = tok_seq * blocks
    row_part = w_qkv.shape[0]
    head_cols = D // blocks
    heads_dev = HEADS // blocks
    unit_dev = FF // blocks
    scale_factor = HEAD_DIM ** (-0.5)
    f32, bf16 = jnp.float32, jnp.bfloat16

    order = ring_order(blocks)
    places = jnp.array([order.index(i) for i in range(blocks)], jnp.int32)
    place = places[block]
    ring_block = jnp.array(order, jnp.int32)[(place + jnp.arange(blocks)) % blocks]
    positions = ring_block[:, None] * tok_seq + jnp.arange(tok_seq, dtype=jnp.int32)[None, :]

    own_x = inputs.reshape(own_rows, D)
    own_cot = cotangent.reshape(own_rows, D)

    qkv_part = lax.dynamic_slice_in_dim(
        w_qkv.reshape(row_part, 3, D), block * head_cols, head_cols, 2
    ).reshape(row_part, 3 * head_cols)
    in_part = jnp.concatenate(
        [
            lax.dynamic_slice_in_dim(w_in, block * unit_dev, unit_dev, 1),
            lax.dynamic_slice_in_dim(w_in, FF + block * unit_dev, unit_dev, 1),
        ],
        axis=1,
    )
    gains = jnp.pad(jnp.stack([gain_one, gain_two], axis=1), ((0, 0), (0, 126)))
    packed = jnp.concatenate([qkv_part, gains], axis=1)
    packed = lax.all_gather(packed, "fsdp", axis=0, tiled=True)
    qkv_c = packed[:, : 3 * head_cols]
    full_g1 = packed[:, 3 * head_cols].astype(f32)
    full_g2 = packed[:, 3 * head_cols + 1].astype(f32)
    all_x = gather_tokens(own_x)
    full_attn = lax.all_gather(w_attn, "fsdp", axis=0, tiled=True)
    in_c = lax.all_gather(in_part, "fsdp", axis=0, tiled=True)
    ffn_cols = lax.all_to_all(w_ffn, "fsdp", split_axis=1, concat_axis=0, tiled=True)
    ffn_c = lax.all_gather(
        lax.dynamic_slice_in_dim(ffn_cols, block * unit_dev, unit_dev, 0),
        "fsdp",
        axis=1,
        tiled=True,
    )
    all_x, later_cot = lax.optimization_barrier((all_x, own_cot))
    all_cot = gather_tokens(later_cot)

    normed_all, _ = norm_parts(all_x.astype(f32))
    input_one = (normed_all * full_g1).astype(bf16)
    project = jnp.dot(input_one, qkv_c, preferred_element_type=f32)
    cosine, sine_part = rotary_tables(positions.reshape(seq_len))
    shaped = project.reshape(blocks, seq_dev, tok_seq, 3, heads_dev, HEAD_DIM)
    shaped = shaped.transpose(3, 1, 0, 2, 4, 5).reshape(3, seq_dev, seq_len, heads_dev, HEAD_DIM)
    queries = rotate(shaped[0], cosine, sine_part).astype(bf16)
    key_rows = rotate(shaped[1], cosine, sine_part).astype(bf16)
    value_rows = shaped[2].astype(bf16)
    scores = (
        jnp.einsum("bthd,bshd->bhts", queries, key_rows, preferred_element_type=f32) * scale_factor
    )
    row_max = jnp.max(scores, axis=-1, keepdims=True)
    exp_vals = jnp.exp(scores - row_max)
    row_sum = jnp.sum(exp_vals, axis=-1, keepdims=True)
    weighted = jnp.einsum(
        "bhts,bshd->bhtd", exp_vals.astype(bf16), value_rows, preferred_element_type=f32
    )
    attn_f = weighted / row_sum
    log_sum = row_max + jnp.log(row_sum)
    attn_b = attn_f.astype(bf16).reshape(seq_dev, heads_dev, blocks, tok_seq, HEAD_DIM)
    attn_b = attn_b.transpose(2, 0, 3, 1, 4).reshape(blocks, own_rows, head_cols)
    by_block = jnp.take(attn_b, (places - place) % blocks, axis=0)
    own_attn = lax.all_to_all(by_block, "ctx", split_axis=0, concat_axis=0, tiled=True)
    own_attn = own_attn.transpose(1, 0, 2).reshape(own_rows, D)

    resid = own_x.astype(f32) + jnp.dot(own_attn, full_attn, preferred_element_type=f32)
    normed_two, inv_two = norm_parts(resid)
    input_two = gather_tokens((normed_two * full_g2).astype(bf16))

    widened = jnp.dot(input_two, in_c, preferred_element_type=f32)
    inner_part = widened[:, :unit_dev]
    gating = widened[:, unit_dev:]
    activated = jax.nn.gelu(inner_part, approximate=False)
    hidden = (activated * gating).astype(bf16)
    grad_hidden = lax.dot_general(
        all_cot, ffn_c, (((1,), (1,)), ((), ())), preferred_element_type=f32
    )
    grad_wide = jnp.concatenate(
        [grad_hidden * gating * gelu_slope(inner_part), grad_hidden * activated], axis=-1
    ).astype(bf16)
    grad_ffn = lax.dot_general(
        hidden, all_cot, (((0,), (0,)), ((), ())), preferred_element_type=f32
    ).astype(bf16)
    grad_in = lax.dot_general(
        grad_wide, input_two, (((0,), (0,)), ((), ())), preferred_element_type=f32
    ).astype(bf16)
    part_two = lax.dot_general(
        grad_wide, in_c, (((1,), (1,)), ((), ())), preferred_element_type=f32
    )
    part_two, grad_ffn, grad_in = lax.optimization_barrier((part_two, grad_ffn, grad_in))
    grad_ffn = lax.psum_scatter(grad_ffn, "fsdp", scatter_dimension=1, tiled=True)
    grad_in = lax.psum_scatter(grad_in, "fsdp", scatter_dimension=1, tiled=True)
    grad_in = lax.all_gather(grad_in, "ctx", axis=0, tiled=False)
    grad_in = grad_in.reshape(blocks, 2, unit_dev, row_part).transpose(1, 0, 2, 3)
    grad_in = grad_in.reshape(2 * FF, row_part).T.astype(f32)
    own_grad_two = scatter_tokens(part_two)

    own_resid = own_cot.astype(f32) + norm_back(own_grad_two * full_g2, normed_two, inv_two)
    resid_b = own_resid.astype(bf16)
    all_resid = gather_tokens(resid_b)
    all_resid, later_hidden, grad_ffn = lax.optimization_barrier((all_resid, hidden, grad_ffn))
    output = resid + scatter_tokens(jnp.dot(later_hidden, ffn_c, preferred_element_type=f32))
    block_of = (places - place) % blocks
    grad_ffn = jnp.take(gather_tokens(grad_ffn).reshape(blocks, unit_dev, -1), block_of, axis=0)
    grad_ffn = grad_ffn.reshape(FF, row_part)
    grad_ffn = lax.all_to_all(grad_ffn, "fsdp", split_axis=0, concat_axis=1, tiled=True)
    grad_ffn = grad_ffn.astype(f32)
    attn_c = lax.dynamic_slice_in_dim(full_attn, block * head_cols, head_cols, 0)
    mixed = lax.dot_general(
        all_resid, attn_c, (((1,), (1,)), ((), ())), preferred_element_type=f32
    ).astype(bf16)
    mixed = mixed.reshape(blocks, seq_dev, tok_seq, heads_dev, HEAD_DIM).transpose(1, 3, 0, 2, 4)
    mixed = mixed.reshape(seq_dev, heads_dev, seq_len, HEAD_DIM)
    grad_attn = lax.dot_general(
        attn_b.reshape(all_rows, head_cols),
        all_resid,
        (((0,), (0,)), ((), ())),
        preferred_element_type=f32,
    ).astype(bf16)

    row_delta = jnp.sum(mixed.astype(f32) * attn_f, axis=-1, keepdims=True)
    probs = jnp.exp(scores - log_sum)
    grad_values = jnp.einsum(
        "bhts,bhtd->bshd", probs.astype(bf16), mixed, preferred_element_type=f32
    )
    grad_probs = jnp.einsum("bhtd,bshd->bhts", mixed, value_rows, preferred_element_type=f32)
    grad_scores = (probs * (grad_probs - row_delta)).astype(bf16)
    grad_query = (
        jnp.einsum("bhts,bshd->bthd", grad_scores, key_rows, preferred_element_type=f32)
        * scale_factor
    )
    grad_keys = (
        jnp.einsum("bhts,bthd->bshd", grad_scores, queries, preferred_element_type=f32)
        * scale_factor
    )
    joint = jnp.stack(
        [
            rotate_back(grad_query, cosine, sine_part),
            rotate_back(grad_keys, cosine, sine_part),
            grad_values,
        ]
    ).astype(bf16)
    joint = joint.reshape(3, seq_dev, blocks, tok_seq, head_cols).transpose(2, 1, 3, 0, 4)
    joint = joint.reshape(all_rows, 3 * head_cols)
    own_grad_one = scatter_tokens(
        lax.dot_general(joint, qkv_c, (((1,), (1,)), ((), ())), preferred_element_type=f32)
    )
    grad_qkv = lax.dot_general(
        joint, input_one, (((0,), (0,)), ((), ())), preferred_element_type=f32
    ).astype(bf16)
    grads = jnp.concatenate([grad_qkv, grad_attn])
    grads = lax.psum_scatter(grads, "fsdp", scatter_dimension=1, tiled=True)
    grads = jnp.take(gather_tokens(grads).reshape(blocks, -1, row_part), block_of, axis=0)
    grad_qkv = grads[:, : 3 * head_cols].reshape(blocks, 3, head_cols, row_part)
    grad_qkv = grad_qkv.transpose(1, 0, 2, 3).reshape(3 * D, row_part).T.astype(f32)
    grad_attn = grads[:, 3 * head_cols :].reshape(D, row_part)
    grad_attn = lax.all_to_all(grad_attn, "fsdp", split_axis=0, concat_axis=1, tiled=True)
    grad_attn = grad_attn.astype(f32)
    normed_one, inv_one = norm_parts(own_x.astype(f32))
    grad_input = own_resid + norm_back(own_grad_one * full_g1, normed_one, inv_one)

    grad_g1 = jnp.sum(w_qkv.astype(f32) * grad_qkv, axis=1) / gain_one.astype(f32)
    grad_g2 = jnp.sum(w_in.astype(f32) * grad_in, axis=1) / gain_two.astype(f32)
    return (
        output.astype(bf16).reshape(seq_dev, tok_seq, D),
        grad_input.reshape(seq_dev, tok_seq, D),
        grad_g1,
        grad_qkv,
        grad_attn,
        grad_g2,
        grad_in,
        grad_ffn,
    )


def solution(mesh):
    blocks = mesh.shape["ctx"]
    split_ok = blocks % 4 == 0 and HEADS % blocks == 0 and FF % blocks == 0 and (D // blocks) % 128 == 0

    return jax.shard_map(
        by_heads if split_ok else on_device,
        mesh=mesh,
        in_specs=(
            P("fsdp", "ctx", None),
            P("fsdp"),
            P("fsdp", None),
            P("fsdp", None),
            P("fsdp"),
            P("fsdp", None),
            P("fsdp", None),
            P("fsdp", "ctx", None),
        ),
        out_specs=(
            P("fsdp", "ctx", None),
            P("fsdp", "ctx", None),
            P("fsdp"),
            P("fsdp", None),
            P("fsdp", None),
            P("fsdp"),
            P("fsdp", None),
            P("fsdp", None),
        ),
        check_vma=False,
    )
```
